256 devices in a mesh: seq: 64 (over y, z_hi, x), ch: 4 (over z_lo, core).
Axes of the slice: x: 4, y: 4, z: 8 (z_hi: 4, z_lo: 2; z = z_hi * 2 + z_lo), core: 2. Of those that a mesh axis runs over, the one named last changes fastest.
Arguments:
- features: bfloat16 [16384, 3, 2048], P('seq', None, 'ch'), may hold values from -6 to 6
- short_weight: float32 [3, 3, 2048], P(None, None, 'ch'), may hold values from -3 to 3
- residue: float32 [2048, 16], P('ch'), may hold values from -1.5 to 1.5
- decay_rate: float32 [2048, 16], P('ch'), may hold values from 1.5258789e-05 to 0.04
- skip_gain: float32 [2048], P('ch'), may hold values from -2.5 to 2.5
- out_weight: bfloat16 [2048, 4096], P('ch'), may hold values from -0.125 to 0.125
- out_grad: bfloat16 [16384, 4096], P('seq', 'ch'), may hold values from -6 to 6
Outputs:
- block_out: bfloat16 [16384, 4096], P('seq', 'ch')
- feature_grad: bfloat16 [16384, 3, 2048], P('seq', None, 'ch')
- short_grad: float32 [3, 3, 2048], P(None, None, 'ch')
- residue_grad: float32 [2048, 16], P('ch')
- skip_grad: float32 [2048], P('ch')
- weight_grad: bfloat16 [4096, 2048], P('seq', 'ch')
The draws below stay inside these ranges and needn't reach their ends.
All inputs are finite; a program needn't handle non-finite values.
Results may differ from the reference program's by a relative error of at most 0.012.
Values may be sent and summed in bfloat16 or wider, within the bound.
No kernel may reach another device: no remote copies, remote signals or barrier semaphores. Data moves between devices by JAX's collectives and lax.ppermute only.
A program may use at most 128 MiB of HBM per device.

```python
import math
import jax
import jax.numpy as jnp
from jax import lax

D = 4096
HC = 2048
RK = 16
KS = 3
TOKENS = 16384


def block_scale(stream_key, shape, split, smallest, top_value):
    loudness = 1.0
    for position, blocks in split:
        steps = jax.random.uniform(jax.random.fold_in(jax.random.fold_in(stream_key, 6), position), (blocks,), jnp.float32, smallest / len(split), top_value / len(split))
        loudness = loudness * jnp.repeat(jnp.exp(steps), shape[position] // blocks).reshape((-1,) + (1,) * (len(shape) - 1 - position))
    return loudness


def scatter_about(rng, shape, width, most, shards=(), held_as=jnp.bfloat16):
    values = jax.random.normal(rng, shape, jnp.float32) * width
    if len(shards) > 0:
        values = block_scale(rng, shape, shards, -0.22, 0.18) * values
    return jnp.clip(values, min=-most, max=most).astype(held_as)


def setup_inputs(seed: int = 0) -> dict:
    splits = jax.random.split(jax.random.key(seed), 8)
    features = scatter_about(splits[0], (TOKENS, 3, HC), 1.0, 6.0, ((0, 64), (2, 4)))
    short_weight = scatter_about(splits[1], (3, KS, HC), 0.6, 3.0, ((2, 4),), jnp.float32)
    residue = scatter_about(splits[2], (HC, RK), 0.25, 1.5, ((0, 4),), jnp.float32)
    decay_rate = jnp.clip(jnp.exp(math.log(0.04) - 7.871479 * jax.random.uniform(splits[3], (HC, RK), jnp.float32) ** block_scale(splits[3], (HC, RK), ((0, 4),), -0.2, 0.2)), 1.52587890625e-05, 0.04)
    skip_gain = scatter_about(splits[4], (HC,), 0.5, 2.5, ((0, 4),), jnp.float32)
    out_weight = scatter_about(splits[5], (HC, D), HC ** -0.5, 0.125, ((0, 4),))
    out_grad = scatter_about(splits[6], (TOKENS, D), 1.0, 6.0, ((0, 64), (1, 4)))
    return dict(features=features, short_weight=short_weight, residue=residue, decay_rate=decay_rate, skip_gain=skip_gain, out_weight=out_weight, out_grad=out_grad)


def causal_block(signal, residue, decay_rate):
    length = signal.shape[1]
    times = jnp.arange(length).astype(jnp.float32)
    powers = jnp.exp(-decay_rate[:, :, None] * times)
    amplitude = residue * jnp.sqrt(2.0 * decay_rate)
    kernel = jnp.einsum('cr,crt->ct', amplitude, powers)
    spectrum = jnp.fft.rfft(kernel, n=2 * length) * jnp.fft.rfft(signal, n=2 * length)
    return jnp.fft.irfft(spectrum, n=2 * length)[:, :length]

def anticausal_block(signal, residue, decay_rate):
    return causal_block(signal[:, ::-1], residue, decay_rate)[:, ::-1]

def correlation_block(gradient, signal, residue, decay_rate):
    length = signal.shape[1]
    spectrum = jnp.fft.rfft(gradient, n=2 * length) * jnp.conj(jnp.fft.rfft(signal, n=2 * length))
    lagged = jnp.fft.irfft(spectrum, n=2 * length)[:, :length]
    times = jnp.arange(length).astype(jnp.float32)
    powers = jnp.exp(-decay_rate[:, :, None] * times)
    return jnp.sqrt(2.0 * decay_rate) * jnp.einsum('ct,crt->cr', lagged, powers)

def by_channels(work, fields, params):
    channels = fields[0].shape[1]
    length = fields[0].shape[0]
    group = min(32, channels)
    stacked = [field.T.reshape(channels // group, group, length) for field in fields]
    grouped = [param.reshape(channels // group, group, param.shape[1]) for param in params]
    return lax.map(lambda items: work(*items), tuple(stacked + grouped))

def reference(features, short_weight, residue, decay_rate, skip_gain, out_weight, out_grad):
    tokens = features.shape[0]
    channels = features.shape[2]
    kernel_taps = short_weight.shape[1]
    grad_scale = 1.0 / math.sqrt(TOKENS)
    feature_float = features.astype(jnp.float32)
    padded = jnp.concatenate([jnp.zeros((kernel_taps - 1, 3, channels), jnp.float32), feature_float], axis=0)
    filtered = jnp.zeros_like(feature_float)
    for shift_index in range(kernel_taps):
        start_row = kernel_taps - 1 - shift_index
        filtered = filtered + short_weight[:, shift_index, :] * padded[start_row:start_row + tokens]
    queries = filtered[:, 0]
    key_field = filtered[:, 1]
    value_field = filtered[:, 2]
    product = (key_field * value_field).astype(jnp.bfloat16)
    product_float = product.astype(jnp.float32)
    conv_part = by_channels(causal_block, [product_float], [residue, decay_rate]).reshape(channels, tokens).T
    gated_mix = (conv_part + skip_gain * product_float).astype(jnp.bfloat16)
    gated_float = gated_mix.astype(jnp.float32)
    mixed_out = (queries * gated_float).astype(jnp.bfloat16)
    block_out = jnp.dot(mixed_out, out_weight, preferred_element_type=jnp.float32).astype(jnp.bfloat16)
    mixed_grad = lax.dot_general(out_grad, out_weight, (((1,), (1,)), ((), ())), preferred_element_type=jnp.float32)
    gate_grad = (mixed_grad * queries).astype(jnp.bfloat16)
    gate_float = gate_grad.astype(jnp.float32)
    query_grad = mixed_grad * gated_float
    back_part = by_channels(anticausal_block, [gate_float], [residue, decay_rate]).reshape(channels, tokens).T
    product_grad = (back_part + skip_gain * gate_float).astype(jnp.bfloat16)
    product_back = product_grad.astype(jnp.float32)
    filtered_grad = jnp.stack([query_grad, product_back * value_field, product_back * key_field], axis=1)
    padded_grad = jnp.concatenate([filtered_grad, jnp.zeros((kernel_taps - 1, 3, channels), jnp.float32)], axis=0)
    feature_grad = jnp.zeros_like(filtered_grad)
    short_terms = []
    for shift_index in range(kernel_taps):
        start_row = kernel_taps - 1 - shift_index
        feature_grad = feature_grad + short_weight[:, shift_index, :] * padded_grad[shift_index:shift_index + tokens]
        short_terms.append(lax.optimization_barrier(jnp.sum(filtered_grad * padded[start_row:start_row + tokens], axis=0)))
    short_grad = jnp.stack(short_terms, axis=1) * grad_scale
    residue_grad = by_channels(correlation_block, [gate_float, product_float], [residue, decay_rate]).reshape(channels, residue.shape[1]) * grad_scale
    skip_grad = lax.optimization_barrier(jnp.sum(gate_float * product_float, axis=0)) * grad_scale
    weight_grad = (lax.dot_general(out_grad, mixed_out, (((0,), (0,)), ((), ())), preferred_element_type=jnp.float32) * grad_scale).astype(jnp.bfloat16)
    return (block_out, feature_grad.astype(jnp.bfloat16), short_grad, residue_grad, skip_grad, weight_grad)
```

```python
import functools
import math

import jax
import jax.numpy as jnp
from jax import lax
from jax.experimental import pallas as pl
from jax.experimental.pallas import tpu as pltpu
from jax.sharding import PartitionSpec as P

F32 = jnp.float32
BF16 = jnp.bfloat16
CHUNKS = 8
LANES = 128
STRIDES = {"x": 1, "z": 4, "y": 16}


def digit(name):
    return (lax.axis_index("seq") // STRIDES[name]) % 4


def ring(block, name, step):
    stride = STRIDES[name]
    route = []
    for source in range(64):
        place = (source // stride) % 4
        route.append((source, source + ((place + step) % 4 - place) * stride))
    return lax.ppermute(block, "seq", route)


def flip_ch(block, mask):
    return lax.ppermute(block, "ch", [(i, i ^ mask) for i in range(4)])


def from_behind(block, distance):
    route = [(i - distance, i) for i in range(64) if 0 <= i - distance < 64]
    return lax.ppermute(block, "seq", route)


def step_rows(index, steps, reverse):
    offset = steps - 1 - index if reverse else index
    return pl.ds(offset, CHUNKS, stride=steps)


def shifted(rows, places, order, reverse):
    moved = pltpu.roll(rows, CHUNKS - places if reverse else places, 0)
    return jnp.where(order >= places, moved, 0.0)


def state_kernel(signal_ref, rate_ref, entry_ref, total_ref, *, reverse):
    steps = signal_ref.shape[0] // CHUNKS
    modes = rate_ref.shape[0]
    order = lax.broadcasted_iota(jnp.int32, (CHUNKS, LANES), 0)
    if reverse:
        order = CHUNKS - 1 - order
    decay = [
        jnp.exp(jnp.broadcast_to(-rate_ref[pl.ds(r, 1), :], (CHUNKS, LANES))) for r in range(modes)
    ]

    def advance(index, states):
        row = signal_ref[step_rows(index, steps, reverse), :]
        return tuple(decay[r] * states[r] + row for r in range(modes))

    zero = jnp.zeros((CHUNKS, LANES), F32)
    states = lax.fori_loop(0, steps, advance, (zero,) * modes, unroll=4)
    last = 0 if reverse else CHUNKS - 1
    for r in range(modes):
        rate = rate_ref[pl.ds(r, 1), :]
        prefix = states[r]
        for places in (1, 2, 4):
            prefix = prefix + jnp.exp(-rate * (places * steps)) * shifted(
                prefix, places, order, reverse
            )
        entry_ref[r] = shifted(prefix, 1, order, reverse)
        total_ref[pl.ds(r, 1), :] = prefix[last : last + 1]


def entry_states(entry_ref, incoming_ref, rate_ref, steps, reverse):
    order = lax.broadcasted_iota(jnp.int32, (CHUNKS, LANES), 0)
    if reverse:
        order = CHUNKS - 1 - order
    span = (order * steps).astype(F32)
    states = []
    for r in range(rate_ref.shape[0]):
        fade = jnp.exp(-rate_ref[pl.ds(r, 1), :] * span)
        states.append(entry_ref[r] + fade * incoming_ref[pl.ds(r, 1), :])
    return tuple(states)


def mode_sum(terms):
    while len(terms) > 1:
        terms = [a + b for a, b in zip(terms[::2], terms[1::2])]
    return terms[0]


def forward_kernel(signal_ref, rate_ref, amp_ref, skip_ref, entry_ref, incoming_ref, out_ref):
    steps = signal_ref.shape[0] // CHUNKS
    modes = rate_ref.shape[0]
    wide = (CHUNKS, LANES)
    decay = [jnp.exp(jnp.broadcast_to(-rate_ref[pl.ds(r, 1), :], wide)) for r in range(modes)]
    amp = [jnp.broadcast_to(amp_ref[pl.ds(r, 1), :], wide) for r in range(modes)]
    skip = jnp.broadcast_to(skip_ref[...], wide)

    def advance(index, states):
        rows = step_rows(index, steps, False)
        row = signal_ref[rows, :]
        states = tuple(decay[r] * states[r] + row for r in range(modes))
        out_ref[rows, :] = mode_sum([amp[r] * states[r] for r in range(modes)]) + skip * row
        return states

    start = entry_states(entry_ref, incoming_ref, rate_ref, steps, False)
    lax.fori_loop(0, steps, advance, start, unroll=2)


def backward_kernel(
    signal_ref, other_ref, rate_ref, amp_ref, skip_ref, entry_ref, incoming_ref, out_ref, dot_ref
):
    steps = signal_ref.shape[0] // CHUNKS
    modes = rate_ref.shape[0]
    wide = (CHUNKS, LANES)
    decay = [jnp.exp(jnp.broadcast_to(-rate_ref[pl.ds(r, 1), :], wide)) for r in range(modes)]
    amp = [jnp.broadcast_to(amp_ref[pl.ds(r, 1), :], wide) for r in range(modes)]
    skip = jnp.broadcast_to(skip_ref[...], wide)

    def advance(index, carry):
        states, sums, direct = carry
        rows = step_rows(index, steps, True)
        row = signal_ref[rows, :]
        other = other_ref[rows, :]
        states = tuple(decay[r] * states[r] + row for r in range(modes))
        out_ref[rows, :] = mode_sum([amp[r] * states[r] for r in range(modes)]) + skip * row
        sums = tuple(sums[r] + other * states[r] for r in range(modes))
        return states, sums, direct + row * other

    zero = jnp.zeros(wide, F32)
    start = entry_states(entry_ref, incoming_ref, rate_ref, steps, True)
    _, sums, direct = lax.fori_loop(0, steps, advance, (start, (zero,) * modes, zero), unroll=2)
    for r in range(modes):
        dot_ref[pl.ds(r, 1), :] = jnp.sum(sums[r], axis=0, keepdims=True)
    dot_ref[pl.ds(modes, 1), :] = jnp.sum(direct, axis=0, keepdims=True)


def column(rows):
    return pl.BlockSpec((rows, LANES), lambda i: (0, i))


def entry_spec(modes):
    return pl.BlockSpec((modes, CHUNKS, LANES), lambda i: (0, 0, i))


def local_states(signal, rate, reverse):
    rows, channels = signal.shape
    modes = rate.shape[0]
    return pl.pallas_call(
        functools.partial(state_kernel, reverse=reverse),
        grid=(channels // LANES,),
        in_specs=[column(rows), column(modes)],
        out_specs=[entry_spec(modes), column(modes)],
        out_shape=[
            jax.ShapeDtypeStruct((modes, CHUNKS, channels), F32),
            jax.ShapeDtypeStruct((modes, channels), F32),
        ],
    )(signal, rate)


def forward_apply(signal, rate, amp, skip, entry, incoming):
    rows, channels = signal.shape
    modes = rate.shape[0]
    return pl.pallas_call(
        forward_kernel,
        grid=(channels // LANES,),
        in_specs=[
            column(rows),
            column(modes),
            column(modes),
            column(1),
            entry_spec(modes),
            column(modes),
        ],
        out_specs=column(rows),
        out_shape=jax.ShapeDtypeStruct((rows, channels), F32),
    )(signal, rate, amp, skip, entry, incoming)


def backward_apply(signal, other, rate, amp, skip, entry, incoming):
    rows, channels = signal.shape
    modes = rate.shape[0]
    return pl.pallas_call(
        backward_kernel,
        grid=(channels // LANES,),
        in_specs=[
            column(rows),
            column(rows),
            column(modes),
            column(modes),
            column(1),
            entry_spec(modes),
            column(modes),
        ],
        out_specs=[column(rows), column(modes + 1)],
        out_shape=[
            jax.ShapeDtypeStruct((rows, channels), F32),
            jax.ShapeDtypeStruct((modes + 1, channels), F32),
        ],
    )(signal, other, rate, amp, skip, entry, incoming)


def entering(total, rate, rows, reverse):
    direction = -1 if reverse else 1
    span = rows
    passed = jnp.zeros((), jnp.int32)
    result = jnp.zeros_like(total)
    for name in ("x", "z", "y"):
        place = digit(name)
        if reverse:
            place = 3 - place
        pieces = [total] + [ring(total, name, direction * k) for k in (1, 2, 3)]
        before = jnp.zeros_like(total)
        whole = jnp.zeros_like(total)
        for k in range(4):
            if k:
                fade = jnp.exp(-rate * (span * (k - 1)))
                before = before + jnp.where(place >= k, fade * pieces[k], 0.0)
            gap = (3 - (place - k) % 4) * span
            whole = whole + jnp.exp(-rate * gap.astype(F32)) * pieces[k]
        result = result + jnp.exp(-rate * passed.astype(F32)) * before
        passed = passed + place * span
        total = whole
        span = span * 4
    return result


def sum_over_seq(block):
    for name in ("x", "z", "y"):
        pieces = [ring(block, name, k) for k in (1, 2, 3)]
        block = (block + pieces[0]) + (pieces[1] + pieces[2])
    return block


def gather_ch(block):
    chip = flip_ch(block, 2)
    core = flip_ch(block, 1)
    both = flip_ch(chip, 1)
    return [block, core, chip, both]


def body(features, short_weight, residue, decay_rate, skip_gain, out_weight, out_grad):
    rows = features.shape[0]
    channels = features.shape[2]
    taps = short_weight.shape[1]
    width = out_grad.shape[1]
    grad_scale = 1.0 / math.sqrt(rows * 64)
    ch = lax.axis_index("ch")
    here = lax.axis_index("seq")

    rate = decay_rate.T
    norm = jnp.sqrt(2.0 * rate)
    amp = residue.T * norm
    skip = skip_gain[None, :]

    before = from_behind(features[rows - (taps - 1) :], 1)
    grad_pieces = gather_ch(out_grad)

    route = []
    for source in range(256):
        s, j = divmod(source, 4)
        y = s // 16
        route.append((source, (s - 16 * y + 16 * j) * 4 + y))
    turned = lax.ppermute(out_grad, ("seq", "ch"), route)

    padded = jnp.concatenate([before, features], axis=0).astype(F32)
    streams = [padded[:, i] for i in range(3)]
    filtered = []
    for i in range(3):
        total = jnp.zeros((rows, channels), F32)
        for j in range(taps):
            start = taps - 1 - j
            total = total + short_weight[i, j] * streams[i][start : start + rows]
        filtered.append(total)
    queries, keys, values = filtered
    product = (keys * values).astype(BF16).astype(F32)

    entry, total = local_states(product, rate, False)
    incoming = entering(total, rate, rows, False)

    def weight_block(mask):
        return lax.dynamic_slice_in_dim(out_weight, (ch ^ mask) * width, width, 1)

    mixed_grad = jnp.zeros((rows, channels), F32)
    for mask in range(4):
        mixed_grad = mixed_grad + lax.dot_general(
            grad_pieces[mask],
            weight_block(mask),
            (((1,), (1,)), ((), ())),
            preferred_element_type=F32,
        )
    gate_grad = (mixed_grad * queries).astype(BF16).astype(F32)
    back_entry, back_total = local_states(gate_grad, rate, True)

    gated = forward_apply(product, rate, amp, skip, entry, incoming).astype(BF16).astype(F32)
    mixed_out = (queries * gated).astype(BF16)
    query_grad = mixed_grad * gated

    back_incoming = entering(back_total, rate, rows, True)

    def out_block(mask):
        return jnp.dot(mixed_out, weight_block(mask), preferred_element_type=F32)

    sent = jnp.concatenate([out_block(1).astype(BF16), out_block(3).astype(BF16)], axis=0)
    got = flip_ch(sent, 1).astype(F32)
    far = flip_ch((out_block(2) + got[rows:]).astype(BF16), 2)
    block_out = (out_block(0) + got[:rows] + far.astype(F32)).astype(BF16)

    turned_pieces = jnp.concatenate(gather_ch(turned), axis=0)
    y_here = digit("y")
    around = jnp.stack([mixed_out] + [ring(mixed_out, "y", k) for k in (1, 2, 3)], axis=0)
    mixed_pieces = jnp.concatenate(
        [
            lax.dynamic_index_in_dim(around, (y_here - (ch ^ mask)) % 4, 0, False)
            for mask in range(4)
        ],
        axis=0,
    )
    share = lax.dot_general(
        turned_pieces, mixed_pieces, (((0,), (0,)), ((), ())), preferred_element_type=F32
    ).astype(BF16)
    groups = [[16 * y + i for i in range(16)] for y in range(4)]
    shares = lax.all_to_all(
        share, "seq", split_axis=0, concat_axis=0, axis_index_groups=groups, tiled=True
    )
    weight_grad = (
        jnp.sum(shares.reshape(16, width // 16, channels).astype(F32), axis=0) * grad_scale
    ).astype(BF16)

    back, dots = backward_apply(gate_grad, product, rate, amp, skip, back_entry, back_incoming)
    back = back.astype(BF16).astype(F32)
    filtered_grad = [query_grad, back * values, back * keys]
    edge = from_behind(jnp.stack([g[: taps - 1] for g in filtered_grad]), -1)
    feature_grad = []
    short_terms = []
    for i in range(3):
        padded_grad = jnp.concatenate([filtered_grad[i], edge[i]], axis=0)
        grad = jnp.zeros((rows, channels), F32)
        for j in range(taps):
            start = taps - 1 - j
            grad = grad + short_weight[i, j] * padded_grad[j : j + rows]
            short_terms.append(jnp.sum(filtered_grad[i] * streams[i][start : start + rows], axis=0))
        feature_grad.append(grad.astype(BF16))
    modes = rate.shape[0]
    sums = sum_over_seq(jnp.concatenate([dots, jnp.stack(short_terms)], axis=0))
    residue_grad = (sums[:modes] * norm * grad_scale).T
    skip_grad = sums[modes] * grad_scale
    short_grad = (sums[modes + 1 :] * grad_scale).reshape(3, taps, channels)
    return (
        block_out,
        jnp.stack(feature_grad, axis=1),
        short_grad,
        residue_grad,
        skip_grad,
        weight_grad,
    )


def solution(mesh):
    in_specs = (
        P("seq", None, "ch"),
        P(None, None, "ch"),
        P("ch", None),
        P("ch", None),
        P("ch"),
        P("ch", None),
        P("seq", "ch"),
    )
    out_specs = (
        P("seq", "ch"),
        P("seq", None, "ch"),
        P(None, None, "ch"),
        P("ch", None),
        P("ch"),
        P("seq", "ch"),
    )
    return jax.shard_map(body, mesh=mesh, in_specs=in_specs, out_specs=out_specs, check_vma=False)
```

```python
import functools
import math

import jax
import jax.numpy as jnp
from jax import lax
from jax.experimental import pallas as pl
from jax.experimental.pallas import tpu as pltpu
from jax.sharding import PartitionSpec as P

F32 = jnp.float32
BF16 = jnp.bfloat16
CHUNKS = 8
LANES = 128
STRIDES = {"x": 1, "z": 4, "y": 16}


def digit(name):
    return (lax.axis_index("seq") // STRIDES[name]) % 4


def swap(block, name, mask):
    stride = STRIDES[name]
    route = []
    for source in range(64):
        place = (source // stride) % 4
        route.append((source, source + ((place ^ mask) - place) * stride))
    return lax.ppermute(block, "seq", route)


def flip_ch(block, mask):
    return lax.ppermute(block, "ch", [(i, i ^ mask) for i in range(4)])


def from_behind(block, distance):
    route = [(i - distance, i) for i in range(64) if 0 <= i - distance < 64]
    return lax.ppermute(block, "seq", route)


def step_rows(index, steps, reverse):
    offset = steps - 1 - index if reverse else index
    return pl.ds(offset, CHUNKS, stride=steps)


def shifted(rows, places, order, reverse):
    moved = pltpu.roll(rows, CHUNKS - places if reverse else places, 0)
    return jnp.where(order >= places, moved, 0.0)


def state_kernel(signal_ref, rate_ref, entry_ref, total_ref, *, reverse):
    steps = signal_ref.shape[0] // CHUNKS
    modes = rate_ref.shape[0]
    order = lax.broadcasted_iota(jnp.int32, (CHUNKS, LANES), 0)
    if reverse:
        order = CHUNKS - 1 - order
    decay = [
        jnp.exp(jnp.broadcast_to(-rate_ref[pl.ds(r, 1), :], (CHUNKS, LANES))) for r in range(modes)
    ]

    def advance(index, states):
        row = signal_ref[step_rows(index, steps, reverse), :]
        return tuple(decay[r] * states[r] + row for r in range(modes))

    zero = jnp.zeros((CHUNKS, LANES), F32)
    states = lax.fori_loop(0, steps, advance, (zero,) * modes, unroll=4)
    last = 0 if reverse else CHUNKS - 1
    for r in range(modes):
        rate = rate_ref[pl.ds(r, 1), :]
        prefix = states[r]
        for places in (1, 2, 4):
            prefix = prefix + jnp.exp(-rate * (places * steps)) * shifted(
                prefix, places, order, reverse
            )
        entry_ref[r] = shifted(prefix, 1, order, reverse)
        total_ref[pl.ds(r, 1), :] = prefix[last : last + 1]


def entry_states(entry_ref, incoming_ref, rate_ref, steps, reverse):
    order = lax.broadcasted_iota(jnp.int32, (CHUNKS, LANES), 0)
    if reverse:
        order = CHUNKS - 1 - order
    span = (order * steps).astype(F32)
    states = []
    for r in range(rate_ref.shape[0]):
        fade = jnp.exp(-rate_ref[pl.ds(r, 1), :] * span)
        states.append(entry_ref[r] + fade * incoming_ref[pl.ds(r, 1), :])
    return tuple(states)


def mode_sum(terms):
    while len(terms) > 1:
        terms = [a + b for a, b in zip(terms[::2], terms[1::2])]
    return terms[0]


def forward_kernel(signal_ref, rate_ref, amp_ref, skip_ref, entry_ref, incoming_ref, out_ref):
    steps = signal_ref.shape[0] // CHUNKS
    modes = rate_ref.shape[0]
    wide = (CHUNKS, LANES)
    decay = [jnp.exp(jnp.broadcast_to(-rate_ref[pl.ds(r, 1), :], wide)) for r in range(modes)]
    amp = [jnp.broadcast_to(amp_ref[pl.ds(r, 1), :], wide) for r in range(modes)]
    skip = jnp.broadcast_to(skip_ref[...], wide)

    def advance(index, states):
        rows = step_rows(index, steps, False)
        row = signal_ref[rows, :]
        states = tuple(decay[r] * states[r] + row for r in range(modes))
        out_ref[rows, :] = mode_sum([amp[r] * states[r] for r in range(modes)]) + skip * row
        return states

    start = entry_states(entry_ref, incoming_ref, rate_ref, steps, False)
    lax.fori_loop(0, steps, advance, start, unroll=2)


def backward_kernel(
    signal_ref, other_ref, rate_ref, amp_ref, skip_ref, entry_ref, incoming_ref, out_ref, dot_ref
):
    steps = signal_ref.shape[0] // CHUNKS
    modes = rate_ref.shape[0]
    wide = (CHUNKS, LANES)
    decay = [jnp.exp(jnp.broadcast_to(-rate_ref[pl.ds(r, 1), :], wide)) for r in range(modes)]
    amp = [jnp.broadcast_to(amp_ref[pl.ds(r, 1), :], wide) for r in range(modes)]
    skip = jnp.broadcast_to(skip_ref[...], wide)

    def advance(index, carry):
        states, sums, direct = carry
        rows = step_rows(index, steps, True)
        row = signal_ref[rows, :]
        other = other_ref[rows, :]
        states = tuple(decay[r] * states[r] + row for r in range(modes))
        out_ref[rows, :] = mode_sum([amp[r] * states[r] for r in range(modes)]) + skip * row
        sums = tuple(sums[r] + other * states[r] for r in range(modes))
        return states, sums, direct + row * other

    zero = jnp.zeros(wide, F32)
    start = entry_states(entry_ref, incoming_ref, rate_ref, steps, True)
    _, sums, direct = lax.fori_loop(0, steps, advance, (start, (zero,) * modes, zero), unroll=2)
    for r in range(modes):
        dot_ref[pl.ds(r, 1), :] = jnp.sum(sums[r], axis=0, keepdims=True)
    dot_ref[pl.ds(modes, 1), :] = jnp.sum(direct, axis=0, keepdims=True)


def column(rows):
    return pl.BlockSpec((rows, LANES), lambda i: (0, i))


def entry_spec(modes):
    return pl.BlockSpec((modes, CHUNKS, LANES), lambda i: (0, 0, i))


def local_states(signal, rate, reverse):
    rows, channels = signal.shape
    modes = rate.shape[0]
    return pl.pallas_call(
        functools.partial(state_kernel, reverse=reverse),
        grid=(channels // LANES,),
        in_specs=[column(rows), column(modes)],
        out_specs=[entry_spec(modes), column(modes)],
        out_shape=[
            jax.ShapeDtypeStruct((modes, CHUNKS, channels), F32),
            jax.ShapeDtypeStruct((modes, channels), F32),
        ],
    )(signal, rate)


def forward_apply(signal, rate, amp, skip, entry, incoming):
    rows, channels = signal.shape
    modes = rate.shape[0]
    return pl.pallas_call(
        forward_kernel,
        grid=(channels // LANES,),
        in_specs=[
            column(rows),
            column(modes),
            column(modes),
            column(1),
            entry_spec(modes),
            column(modes),
        ],
        out_specs=column(rows),
        out_shape=jax.ShapeDtypeStruct((rows, channels), F32),
    )(signal, rate, amp, skip, entry, incoming)


def backward_apply(signal, other, rate, amp, skip, entry, incoming):
    rows, channels = signal.shape
    modes = rate.shape[0]
    return pl.pallas_call(
        backward_kernel,
        grid=(channels // LANES,),
        in_specs=[
            column(rows),
            column(rows),
            column(modes),
            column(modes),
            column(1),
            entry_spec(modes),
            column(modes),
        ],
        out_specs=[column(rows), column(modes + 1)],
        out_shape=[
            jax.ShapeDtypeStruct((rows, channels), F32),
            jax.ShapeDtypeStruct((modes + 1, channels), F32),
        ],
    )(signal, other, rate, amp, skip, entry, incoming)


def entering(totals, rate, rows):
    span = rows
    passed = jnp.zeros((2, 1, 1), jnp.int32)
    result = jnp.zeros_like(totals)
    for name in ("x", "z", "y"):
        place = digit(name)
        pieces = [totals] + [swap(totals, name, mask) for mask in (1, 2, 3)]
        outside = jnp.zeros_like(totals)
        whole = jnp.zeros_like(totals)
        for mask in range(4):
            source = place ^ mask
            if mask:
                gap = jnp.stack([place - 1 - source, source - 1 - place]).reshape(2, 1, 1)
                fade = jnp.exp(-rate * (jnp.maximum(gap, 0) * span).astype(F32))
                outside = outside + jnp.where(gap >= 0, fade * pieces[mask], 0.0)
            rest = jnp.stack([3 - source, source]).reshape(2, 1, 1)
            whole = whole + jnp.exp(-rate * (rest * span).astype(F32)) * pieces[mask]
        result = result + jnp.exp(-rate * passed.astype(F32)) * outside
        passed = passed + jnp.stack([place, 3 - place]).reshape(2, 1, 1) * span
        totals = whole
        span = span * 4
    return result


def sum_over_seq(block):
    for name in ("x", "z", "y"):
        pieces = [swap(block, name, mask) for mask in (1, 2, 3)]
        block = (block + pieces[0]) + (pieces[1] + pieces[2])
    return block


def gather_ch(block):
    chip = flip_ch(block, 2)
    core = flip_ch(block, 1)
    both = flip_ch(chip, 1)
    return [block, core, chip, both]


def body(features, short_weight, residue, decay_rate, skip_gain, out_weight, out_grad):
    rows = features.shape[0]
    channels = features.shape[2]
    taps = short_weight.shape[1]
    width = out_grad.shape[1]
    grad_scale = 1.0 / math.sqrt(rows * 64)
    ch = lax.axis_index("ch")

    rate = decay_rate.T
    norm = jnp.sqrt(2.0 * rate)
    amp = residue.T * norm
    skip = skip_gain[None, :]

    before = from_behind(features[rows - (taps - 1) :], 1)
    grad_pieces = gather_ch(out_grad)

    route = []
    for source in range(256):
        s, j = divmod(source, 4)
        y = s // 16
        route.append((source, (s - 16 * y + 16 * j) * 4 + y))
    turned = lax.ppermute(out_grad, ("seq", "ch"), route)

    padded = jnp.concatenate([before, features], axis=0).astype(F32)
    streams = [padded[:, i] for i in range(3)]
    filtered = []
    for i in range(3):
        total = jnp.zeros((rows, channels), F32)
        for j in range(taps):
            start = taps - 1 - j
            total = total + short_weight[i, j] * streams[i][start : start + rows]
        filtered.append(total)
    queries, keys, values = filtered
    product = (keys * values).astype(BF16).astype(F32)

    entry, total = local_states(product, rate, False)
    def weight_block(mask):
        return lax.dynamic_slice_in_dim(out_weight, (ch ^ mask) * width, width, 1)

    mixed_grad = jnp.zeros((rows, channels), F32)
    for mask in range(4):
        mixed_grad = mixed_grad + lax.dot_general(
            grad_pieces[mask],
            weight_block(mask),
            (((1,), (1,)), ((), ())),
            preferred_element_type=F32,
        )
    gate_grad = (mixed_grad * queries).astype(BF16).astype(F32)
    back_entry, back_total = local_states(gate_grad, rate, True)
    incoming, back_incoming = entering(jnp.stack([total, back_total]), rate, rows)

    gated = forward_apply(product, rate, amp, skip, entry, incoming).astype(BF16).astype(F32)
    mixed_out = (queries * gated).astype(BF16)
    query_grad = mixed_grad * gated

    def out_block(mask):
        return jnp.dot(mixed_out, weight_block(mask), preferred_element_type=F32)

    sent = jnp.concatenate([out_block(1).astype(BF16), out_block(3).astype(BF16)], axis=0)
    back_incoming, sent = lax.optimization_barrier((back_incoming, sent))
    got = flip_ch(sent, 1).astype(F32)
    far_sent = (out_block(2) + got[rows:]).astype(BF16)

    turned_pieces = jnp.concatenate(gather_ch(turned), axis=0)
    y_here = digit("y")
    around = jnp.stack([mixed_out] + [swap(mixed_out, "y", k) for k in (1, 2, 3)], axis=0)
    mixed_pieces = jnp.concatenate(
        [
            lax.dynamic_index_in_dim(around, y_here ^ ch ^ mask, 0, False)
            for mask in range(4)
        ],
        axis=0,
    )
    share = lax.dot_general(
        turned_pieces, mixed_pieces, (((0,), (0,)), ((), ())), preferred_element_type=F32
    ).astype(BF16)
    groups = [[16 * y + i for i in range(16)] for y in range(4)]
    shares = lax.all_to_all(
        share, "seq", split_axis=0, concat_axis=0, axis_index_groups=groups, tiled=True
    )
    weight_grad = (
        jnp.sum(shares.reshape(16, width // 16, channels).astype(F32), axis=0) * grad_scale
    ).astype(BF16)

    back, dots = backward_apply(gate_grad, product, rate, amp, skip, back_entry, back_incoming)
    back = back.astype(BF16).astype(F32)
    filtered_grad = [query_grad, back * values, back * keys]
    edge = from_behind(jnp.stack([g[: taps - 1] for g in filtered_grad]), -1)
    feature_grad = []
    short_terms = []
    for i in range(3):
        padded_grad = jnp.concatenate([filtered_grad[i], edge[i]], axis=0)
        grad = jnp.zeros((rows, channels), F32)
        for j in range(taps):
            start = taps - 1 - j
            grad = grad + short_weight[i, j] * padded_grad[j : j + rows]
            short_terms.append(jnp.sum(filtered_grad[i] * streams[i][start : start + rows], axis=0))
        feature_grad.append(grad.astype(BF16))
    modes = rate.shape[0]
    parts = jnp.concatenate([dots, jnp.stack(short_terms)], axis=0)
    parts, far_sent = lax.optimization_barrier((parts, far_sent))
    far = flip_ch(far_sent, 2)
    block_out = (out_block(0) + got[:rows] + far.astype(F32)).astype(BF16)
    sums = sum_over_seq(parts)
    residue_grad = (sums[:modes] * norm * grad_scale).T
    skip_grad = sums[modes] * grad_scale
    short_grad = (sums[modes + 1 :] * grad_scale).reshape(3, taps, channels)
    return (
        block_out,
        jnp.stack(feature_grad, axis=1),
        short_grad,
        residue_grad,
        skip_grad,
        weight_grad,
    )


def solution(mesh):
    in_specs = (
        P("seq", None, "ch"),
        P(None, None, "ch"),
        P("ch", None),
        P("ch", None),
        P("ch"),
        P("ch", None),
        P("seq", "ch"),
    )
    out_specs = (
        P("seq", "ch"),
        P("seq", None, "ch"),
        P(None, None, "ch"),
        P("ch", None),
        P("ch"),
        P("seq", "ch"),
    )
    return jax.shard_map(body, mesh=mesh, in_specs=in_specs, out_specs=out_specs, check_vma=False)
```

```python
import functools
import math

import jax
import jax.numpy as jnp
from jax import lax
from jax.experimental import pallas as pl
from jax.experimental.pallas import tpu as pltpu
from jax.sharding import PartitionSpec as P

F32 = jnp.float32
BF16 = jnp.bfloat16
CHUNKS = 8
LANES = 128
STRIDES = {"x": 1, "z": 4, "y": 16}


def digit(name):
    return (lax.axis_index("seq") // STRIDES[name]) % 4


def swap(block, name, mask):
    stride = STRIDES[name]
    route = []
    for source in range(64):
        place = (source // stride) % 4
        route.append((source, source + ((place ^ mask) - place) * stride))
    return lax.ppermute(block, "seq", route)


def flip_ch(block, mask):
    return lax.ppermute(block, "ch", [(i, i ^ mask) for i in range(4)])


def from_behind(block, distance):
    route = [(i - distance, i) for i in range(64) if 0 <= i - distance < 64]
    return lax.ppermute(block, "seq", route)


def step_rows(index, steps, reverse):
    offset = steps - 1 - index if reverse else index
    return pl.ds(offset, CHUNKS, stride=steps)


def shifted(rows, places, order, reverse):
    moved = pltpu.roll(rows, CHUNKS - places if reverse else places, 0)
    return jnp.where(order >= places, moved, 0.0)


def state_kernel(signal_ref, rate_ref, entry_ref, total_ref, *, reverse):
    steps = signal_ref.shape[0] // CHUNKS
    modes = rate_ref.shape[0]
    order = lax.broadcasted_iota(jnp.int32, (CHUNKS, LANES), 0)
    if reverse:
        order = CHUNKS - 1 - order
    decay = [
        jnp.exp(jnp.broadcast_to(-rate_ref[pl.ds(r, 1), :], (CHUNKS, LANES))) for r in range(modes)
    ]

    def advance(index, states):
        row = signal_ref[step_rows(index, steps, reverse), :]
        return tuple(decay[r] * states[r] + row for r in range(modes))

    zero = jnp.zeros((CHUNKS, LANES), F32)
    states = lax.fori_loop(0, steps, advance, (zero,) * modes, unroll=4)
    last = 0 if reverse else CHUNKS - 1
    for r in range(modes):
        rate = rate_ref[pl.ds(r, 1), :]
        prefix = states[r]
        for places in (1, 2, 4):
            prefix = prefix + jnp.exp(-rate * (places * steps)) * shifted(
                prefix, places, order, reverse
            )
        entry_ref[r] = shifted(prefix, 1, order, reverse)
        total_ref[pl.ds(r, 1), :] = prefix[last : last + 1]


def entry_states(entry_ref, incoming_ref, rate_ref, steps, reverse):
    order = lax.broadcasted_iota(jnp.int32, (CHUNKS, LANES), 0)
    if reverse:
        order = CHUNKS - 1 - order
    span = (order * steps).astype(F32)
    states = []
    for r in range(rate_ref.shape[0]):
        fade = jnp.exp(-rate_ref[pl.ds(r, 1), :] * span)
        states.append(entry_ref[r] + fade * incoming_ref[pl.ds(r, 1), :])
    return tuple(states)


def mode_sum(terms):
    while len(terms) > 1:
        terms = [a + b for a, b in zip(terms[::2], terms[1::2])]
    return terms[0]


def forward_kernel(signal_ref, rate_ref, amp_ref, skip_ref, entry_ref, incoming_ref, out_ref):
    steps = signal_ref.shape[0] // CHUNKS
    modes = rate_ref.shape[0]
    wide = (CHUNKS, LANES)
    decay = [jnp.exp(jnp.broadcast_to(-rate_ref[pl.ds(r, 1), :], wide)) for r in range(modes)]
    amp = [jnp.broadcast_to(amp_ref[pl.ds(r, 1), :], wide) for r in range(modes)]
    skip = jnp.broadcast_to(skip_ref[...], wide)

    def advance(index, states):
        rows = step_rows(index, steps, False)
        row = signal_ref[rows, :]
        states = tuple(decay[r] * states[r] + row for r in range(modes))
        out_ref[rows, :] = mode_sum([amp[r] * states[r] for r in range(modes)]) + skip * row
        return states

    start = entry_states(entry_ref, incoming_ref, rate_ref, steps, False)
    lax.fori_loop(0, steps, advance, start, unroll=2)


def backward_kernel(
    signal_ref, other_ref, rate_ref, amp_ref, skip_ref, entry_ref, incoming_ref, out_ref, dot_ref
):
    steps = signal_ref.shape[0] // CHUNKS
    modes = rate_ref.shape[0]
    wide = (CHUNKS, LANES)
    decay = [jnp.exp(jnp.broadcast_to(-rate_ref[pl.ds(r, 1), :], wide)) for r in range(modes)]
    amp = [jnp.broadcast_to(amp_ref[pl.ds(r, 1), :], wide) for r in range(modes)]
    skip = jnp.broadcast_to(skip_ref[...], wide)

    def advance(index, carry):
        states, sums, direct = carry
        rows = step_rows(index, steps, True)
        row = signal_ref[rows, :]
        other = other_ref[rows, :]
        states = tuple(decay[r] * states[r] + row for r in range(modes))
        out_ref[rows, :] = mode_sum([amp[r] * states[r] for r in range(modes)]) + skip * row
        sums = tuple(sums[r] + other * states[r] for r in range(modes))
        return states, sums, direct + row * other

    zero = jnp.zeros(wide, F32)
    start = entry_states(entry_ref, incoming_ref, rate_ref, steps, True)
    _, sums, direct = lax.fori_loop(0, steps, advance, (start, (zero,) * modes, zero), unroll=2)
    for r in range(modes):
        dot_ref[pl.ds(r, 1), :] = jnp.sum(sums[r], axis=0, keepdims=True)
    dot_ref[pl.ds(modes, 1), :] = jnp.sum(direct, axis=0, keepdims=True)


def column(rows):
    return pl.BlockSpec((rows, LANES), lambda i: (0, i))


def entry_spec(modes):
    return pl.BlockSpec((modes, CHUNKS, LANES), lambda i: (0, 0, i))


def local_states(signal, rate, reverse):
    rows, channels = signal.shape
    modes = rate.shape[0]
    return pl.pallas_call(
        functools.partial(state_kernel, reverse=reverse),
        grid=(channels // LANES,),
        in_specs=[column(rows), column(modes)],
        out_specs=[entry_spec(modes), column(modes)],
        out_shape=[
            jax.ShapeDtypeStruct((modes, CHUNKS, channels), F32),
            jax.ShapeDtypeStruct((modes, channels), F32),
        ],
    )(signal, rate)


def forward_apply(signal, rate, amp, skip, entry, incoming):
    rows, channels = signal.shape
    modes = rate.shape[0]
    return pl.pallas_call(
        forward_kernel,
        grid=(channels // LANES,),
        in_specs=[
            column(rows),
            column(modes),
            column(modes),
            column(1),
            entry_spec(modes),
            column(modes),
        ],
        out_specs=column(rows),
        out_shape=jax.ShapeDtypeStruct((rows, channels), F32),
    )(signal, rate, amp, skip, entry, incoming)


def backward_apply(signal, other, rate, amp, skip, entry, incoming):
    rows, channels = signal.shape
    modes = rate.shape[0]
    return pl.pallas_call(
        backward_kernel,
        grid=(channels // LANES,),
        in_specs=[
            column(rows),
            column(rows),
            column(modes),
            column(modes),
            column(1),
            entry_spec(modes),
            column(modes),
        ],
        out_specs=[column(rows), column(modes + 1)],
        out_shape=[
            jax.ShapeDtypeStruct((rows, channels), F32),
            jax.ShapeDtypeStruct((modes + 1, channels), F32),
        ],
    )(signal, other, rate, amp, skip, entry, incoming)


def entering(totals, rate, rows):
    span = rows
    passed = jnp.zeros((2, 1, 1), jnp.int32)
    result = jnp.zeros_like(totals)
    for name in ("x", "z", "y"):
        place = digit(name)
        pieces = [totals] + [swap(totals, name, mask) for mask in (1, 2, 3)]
        outside = jnp.zeros_like(totals)
        whole = jnp.zeros_like(totals)
        for mask in range(4):
            source = place ^ mask
            if mask:
                gap = jnp.stack([place - 1 - source, source - 1 - place]).reshape(2, 1, 1)
                fade = jnp.exp(-rate * (jnp.maximum(gap, 0) * span).astype(F32))
                outside = outside + jnp.where(gap >= 0, fade * pieces[mask], 0.0)
            rest = jnp.stack([3 - source, source]).reshape(2, 1, 1)
            whole = whole + jnp.exp(-rate * (rest * span).astype(F32)) * pieces[mask]
        result = result + jnp.exp(-rate * passed.astype(F32)) * outside
        passed = passed + jnp.stack([place, 3 - place]).reshape(2, 1, 1) * span
        totals = whole
        span = span * 4
    return result


def sum_along(block, name):
    pieces = [swap(block, name, mask) for mask in (1, 2, 3)]
    return (block + pieces[0]) + (pieces[1] + pieces[2])


def gather_ch(block):
    chip = flip_ch(block, 2)
    core = flip_ch(block, 1)
    both = flip_ch(chip, 1)
    return [block, core, chip, both]


def body(features, short_weight, residue, decay_rate, skip_gain, out_weight, out_grad):
    rows = features.shape[0]
    channels = features.shape[2]
    taps = short_weight.shape[1]
    width = out_grad.shape[1]
    grad_scale = 1.0 / math.sqrt(rows * 64)
    ch = lax.axis_index("ch")

    rate = decay_rate.T
    norm = jnp.sqrt(2.0 * rate)
    amp = residue.T * norm
    skip = skip_gain[None, :]

    before = from_behind(features[rows - (taps - 1) :], 1)
    grad_pieces = gather_ch(out_grad)

    route = []
    for source in range(256):
        s, j = divmod(source, 4)
        y = s // 16
        route.append((source, (s - 16 * y + 16 * j) * 4 + y))
    before, held_grad = lax.optimization_barrier((before, out_grad))
    turned = lax.ppermute(held_grad, ("seq", "ch"), route)

    padded = jnp.concatenate([before, features], axis=0).astype(F32)
    streams = [padded[:, i] for i in range(3)]
    filtered = []
    for i in range(3):
        total = jnp.zeros((rows, channels), F32)
        for j in range(taps):
            start = taps - 1 - j
            total = total + short_weight[i, j] * streams[i][start : start + rows]
        filtered.append(total)
    queries, keys, values = filtered
    product = (keys * values).astype(BF16).astype(F32)

    entry, total = local_states(product, rate, False)
    def weight_block(mask):
        return lax.dynamic_slice_in_dim(out_weight, (ch ^ mask) * width, width, 1)

    mixed_grad = jnp.zeros((rows, channels), F32)
    for mask in range(4):
        mixed_grad = mixed_grad + lax.dot_general(
            grad_pieces[mask],
            weight_block(mask),
            (((1,), (1,)), ((), ())),
            preferred_element_type=F32,
        )
    gate_grad = (mixed_grad * queries).astype(BF16).astype(F32)
    back_entry, back_total = local_states(gate_grad, rate, True)
    incoming, back_incoming = entering(jnp.stack([total, back_total]), rate, rows)

    gated = forward_apply(product, rate, amp, skip, entry, incoming).astype(BF16).astype(F32)
    mixed_out = (queries * gated).astype(BF16)
    query_grad = mixed_grad * gated

    def out_block(mask):
        return jnp.dot(mixed_out, weight_block(mask), preferred_element_type=F32)

    sent = jnp.concatenate([out_block(1).astype(BF16), out_block(3).astype(BF16)], axis=0)
    back_incoming, sent = lax.optimization_barrier((back_incoming, sent))
    got = flip_ch(sent, 1).astype(F32)
    far_sent = (out_block(2) + got[rows:]).astype(BF16)

    turned_pieces = jnp.concatenate(gather_ch(turned), axis=0)
    y_here = digit("y")
    around = jnp.stack([mixed_out] + [swap(mixed_out, "y", k) for k in (1, 2, 3)], axis=0)
    mixed_pieces = jnp.concatenate(
        [
            lax.dynamic_index_in_dim(around, y_here ^ ch ^ mask, 0, False)
            for mask in range(4)
        ],
        axis=0,
    )

    back, dots = backward_apply(gate_grad, product, rate, amp, skip, back_entry, back_incoming)
    back = back.astype(BF16).astype(F32)
    filtered_grad = [query_grad, back * values, back * keys]
    edge = from_behind(jnp.stack([g[: taps - 1] for g in filtered_grad]), -1)
    feature_grad = []
    short_terms = []
    for i in range(3):
        padded_grad = jnp.concatenate([filtered_grad[i], edge[i]], axis=0)
        grad = jnp.zeros((rows, channels), F32)
        for j in range(taps):
            start = taps - 1 - j
            grad = grad + short_weight[i, j] * padded_grad[j : j + rows]
            short_terms.append(jnp.sum(filtered_grad[i] * streams[i][start : start + rows], axis=0))
        feature_grad.append(grad.astype(BF16))
    modes = rate.shape[0]
    parts = jnp.concatenate([dots, jnp.stack(short_terms)], axis=0)
    parts, mixed_pieces = lax.optimization_barrier((parts, mixed_pieces))
    far = flip_ch(far_sent, 2)
    share = lax.dot_general(
        turned_pieces, mixed_pieces, (((0,), (0,)), ((), ())), preferred_element_type=F32
    ).astype(BF16)
    sums = sum_along(parts, "x")
    sums, far = lax.optimization_barrier((sums, far))
    block_out = (out_block(0) + got[:rows] + far.astype(F32)).astype(BF16)
    sums = sum_along(sums, "z")
    sums, share = lax.optimization_barrier((sums, share))
    groups = [[16 * y + i for i in range(16)] for y in range(4)]
    shares = lax.all_to_all(
        share, "seq", split_axis=0, concat_axis=0, axis_index_groups=groups, tiled=True
    )
    weight_grad = (
        jnp.sum(shares.reshape(16, width // 16, channels).astype(F32), axis=0) * grad_scale
    ).astype(BF16)
    sums = sum_along(sums, "y")
    residue_grad = (sums[:modes] * norm * grad_scale).T
    skip_grad = sums[modes] * grad_scale
    short_grad = (sums[modes + 1 :] * grad_scale).reshape(3, taps, channels)
    return (
        block_out,
        jnp.stack(feature_grad, axis=1),
        short_grad,
        residue_grad,
        skip_grad,
        weight_grad,
    )


def solution(mesh):
    in_specs = (
        P("seq", None, "ch"),
        P(None, None, "ch"),
        P("ch", None),
        P("ch", None),
        P("ch"),
        P("ch", None),
        P("seq", "ch"),
    )
    out_specs = (
        P("seq", "ch"),
        P("seq", None, "ch"),
        P(None, None, "ch"),
        P("ch", None),
        P("ch"),
        P("seq", "ch"),
    )
    return jax.shard_map(body, mesh=mesh, in_specs=in_specs, out_specs=out_specs, check_vma=False)
```

```python
import functools
import math

import jax
import jax.numpy as jnp
from jax import lax
from jax.experimental import pallas as pl
from jax.experimental.pallas import tpu as pltpu
from jax.sharding import PartitionSpec as P

F32 = jnp.float32
BF16 = jnp.bfloat16
CHUNKS = 8
LANES = 128
STRIDES = {"x": 1, "z": 4, "y": 16}


def digit(name):
    return (lax.axis_index("seq") // STRIDES[name]) % 4


def swap(block, name, mask):
    stride = STRIDES[name]
    route = []
    for source in range(64):
        place = (source // stride) % 4
        route.append((source, source + ((place ^ mask) - place) * stride))
    return lax.ppermute(block, "seq", route)


def flip_ch(block, mask):
    return lax.ppermute(block, "ch", [(i, i ^ mask) for i in range(4)])


def from_behind(block, distance):
    route = [(i - distance, i) for i in range(64) if 0 <= i - distance < 64]
    return lax.ppermute(block, "seq", route)


def step_rows(index, steps, reverse):
    offset = steps - 1 - index if reverse else index
    return pl.ds(offset, CHUNKS, stride=steps)


def shifted(rows, places, order, reverse):
    moved = pltpu.roll(rows, CHUNKS - places if reverse else places, 0)
    return jnp.where(order >= places, moved, 0.0)


def state_kernel(signal_ref, rate_ref, entry_ref, total_ref, *, reverse):
    steps = signal_ref.shape[0] // CHUNKS
    modes = rate_ref.shape[0]
    order = lax.broadcasted_iota(jnp.int32, (CHUNKS, LANES), 0)
    if reverse:
        order = CHUNKS - 1 - order
    decay = [
        jnp.exp(jnp.broadcast_to(-rate_ref[pl.ds(r, 1), :], (CHUNKS, LANES))) for r in range(modes)
    ]

    def advance(index, states):
        row = signal_ref[step_rows(index, steps, reverse), :]
        return tuple(decay[r] * states[r] + row for r in range(modes))

    zero = jnp.zeros((CHUNKS, LANES), F32)
    states = lax.fori_loop(0, steps, advance, (zero,) * modes, unroll=4)
    last = 0 if reverse else CHUNKS - 1
    for r in range(modes):
        rate = rate_ref[pl.ds(r, 1), :]
        prefix = states[r]
        for places in (1, 2, 4):
            prefix = prefix + jnp.exp(-rate * (places * steps)) * shifted(
                prefix, places, order, reverse
            )
        entry_ref[r] = shifted(prefix, 1, order, reverse)
        total_ref[pl.ds(r, 1), :] = prefix[last : last + 1]


def entry_states(entry_ref, incoming_ref, rate_ref, steps, reverse):
    order = lax.broadcasted_iota(jnp.int32, (CHUNKS, LANES), 0)
    if reverse:
        order = CHUNKS - 1 - order
    span = (order * steps).astype(F32)
    states = []
    for r in range(rate_ref.shape[0]):
        fade = jnp.exp(-rate_ref[pl.ds(r, 1), :] * span)
        states.append(entry_ref[r] + fade * incoming_ref[pl.ds(r, 1), :])
    return tuple(states)


def mode_sum(terms):
    while len(terms) > 1:
        terms = [a + b for a, b in zip(terms[::2], terms[1::2])]
    return terms[0]


def forward_kernel(signal_ref, rate_ref, amp_ref, skip_ref, entry_ref, incoming_ref, out_ref):
    steps = signal_ref.shape[0] // CHUNKS
    modes = rate_ref.shape[0]
    wide = (CHUNKS, LANES)
    decay = [jnp.exp(jnp.broadcast_to(-rate_ref[pl.ds(r, 1), :], wide)) for r in range(modes)]
    amp = [jnp.broadcast_to(amp_ref[pl.ds(r, 1), :], wide) for r in range(modes)]
    skip = jnp.broadcast_to(skip_ref[...], wide)

    def advance(index, states):
        rows = step_rows(index, steps, False)
        row = signal_ref[rows, :]
        states = tuple(decay[r] * states[r] + row for r in range(modes))
        out_ref[rows, :] = mode_sum([amp[r] * states[r] for r in range(modes)]) + skip * row
        return states

    start = entry_states(entry_ref, incoming_ref, rate_ref, steps, False)
    lax.fori_loop(0, steps, advance, start, unroll=2)


def backward_kernel(
    signal_ref, other_ref, rate_ref, amp_ref, skip_ref, entry_ref, incoming_ref, out_ref, dot_ref
):
    steps = signal_ref.shape[0] // CHUNKS
    modes = rate_ref.shape[0]
    wide = (CHUNKS, LANES)
    decay = [jnp.exp(jnp.broadcast_to(-rate_ref[pl.ds(r, 1), :], wide)) for r in range(modes)]
    amp = [jnp.broadcast_to(amp_ref[pl.ds(r, 1), :], wide) for r in range(modes)]
    skip = jnp.broadcast_to(skip_ref[...], wide)

    def advance(index, carry):
        states, sums, direct = carry
        rows = step_rows(index, steps, True)
        row = signal_ref[rows, :]
        other = other_ref[rows, :]
        states = tuple(decay[r] * states[r] + row for r in range(modes))
        out_ref[rows, :] = mode_sum([amp[r] * states[r] for r in range(modes)]) + skip * row
        sums = tuple(sums[r] + other * states[r] for r in range(modes))
        return states, sums, direct + row * other

    zero = jnp.zeros(wide, F32)
    start = entry_states(entry_ref, incoming_ref, rate_ref, steps, True)
    _, sums, direct = lax.fori_loop(0, steps, advance, (start, (zero,) * modes, zero), unroll=2)
    for r in range(modes):
        dot_ref[pl.ds(r, 1), :] = jnp.sum(sums[r], axis=0, keepdims=True)
    dot_ref[pl.ds(modes, 1), :] = jnp.sum(direct, axis=0, keepdims=True)


def column(rows):
    return pl.BlockSpec((rows, LANES), lambda i: (0, i))


def entry_spec(modes):
    return pl.BlockSpec((modes, CHUNKS, LANES), lambda i: (0, 0, i))


def local_states(signal, rate, reverse):
    rows, channels = signal.shape
    modes = rate.shape[0]
    return pl.pallas_call(
        functools.partial(state_kernel, reverse=reverse),
        grid=(channels // LANES,),
        in_specs=[column(rows), column(modes)],
        out_specs=[entry_spec(modes), column(modes)],
        out_shape=[
            jax.ShapeDtypeStruct((modes, CHUNKS, channels), F32),
            jax.ShapeDtypeStruct((modes, channels), F32),
        ],
    )(signal, rate)


def forward_apply(signal, rate, amp, skip, entry, incoming):
    rows, channels = signal.shape
    modes = rate.shape[0]
    return pl.pallas_call(
        forward_kernel,
        grid=(channels // LANES,),
        in_specs=[
            column(rows),
            column(modes),
            column(modes),
            column(1),
            entry_spec(modes),
            column(modes),
        ],
        out_specs=column(rows),
        out_shape=jax.ShapeDtypeStruct((rows, channels), F32),
    )(signal, rate, amp, skip, entry, incoming)


def backward_apply(signal, other, rate, amp, skip, entry, incoming):
    rows, channels = signal.shape
    modes = rate.shape[0]
    return pl.pallas_call(
        backward_kernel,
        grid=(channels // LANES,),
        in_specs=[
            column(rows),
            column(rows),
            column(modes),
            column(modes),
            column(1),
            entry_spec(modes),
            column(modes),
        ],
        out_specs=[column(rows), column(modes + 1)],
        out_shape=[
            jax.ShapeDtypeStruct((rows, channels), F32),
            jax.ShapeDtypeStruct((modes + 1, channels), F32),
        ],
    )(signal, other, rate, amp, skip, entry, incoming)


def entering(totals, rate, rows):
    span = rows
    passed = jnp.zeros((2, 1, 1), jnp.int32)
    result = jnp.zeros_like(totals)
    for name in ("x", "z", "y"):
        place = digit(name)
        pieces = [totals] + [swap(totals, name, mask) for mask in (1, 2, 3)]
        outside = jnp.zeros_like(totals)
        whole = jnp.zeros_like(totals)
        for mask in range(4):
            source = place ^ mask
            if mask:
                gap = jnp.stack([place - 1 - source, source - 1 - place]).reshape(2, 1, 1)
                fade = jnp.exp(-rate * (jnp.maximum(gap, 0) * span).astype(F32))
                outside = outside + jnp.where(gap >= 0, fade * pieces[mask], 0.0)
            rest = jnp.stack([3 - source, source]).reshape(2, 1, 1)
            whole = whole + jnp.exp(-rate * (rest * span).astype(F32)) * pieces[mask]
        result = result + jnp.exp(-rate * passed.astype(F32)) * outside
        passed = passed + jnp.stack([place, 3 - place]).reshape(2, 1, 1) * span
        totals = whole
        span = span * 4
    return result


def sum_along(block, name):
    pieces = [swap(block, name, mask) for mask in (1, 2, 3)]
    return (block + pieces[0]) + (pieces[1] + pieces[2])


def gather_ch(block):
    chip = flip_ch(block, 2)
    core = flip_ch(block, 1)
    both = flip_ch(chip, 1)
    return [block, core, chip, both]


def body(features, short_weight, residue, decay_rate, skip_gain, out_weight, out_grad):
    rows = features.shape[0]
    channels = features.shape[2]
    taps = short_weight.shape[1]
    width = out_grad.shape[1]
    grad_scale = 1.0 / math.sqrt(rows * 64)
    ch = lax.axis_index("ch")

    rate = decay_rate.T
    norm = jnp.sqrt(2.0 * rate)
    amp = residue.T * norm
    skip = skip_gain[None, :]

    before = from_behind(features[rows - (taps - 1) :], 1)
    grad_pieces = gather_ch(out_grad)

    route = []
    for source in range(256):
        s, j = divmod(source, 4)
        y = s // 16
        route.append((source, (s - 16 * y + 16 * j) * 4 + y))
    before, held_grad = lax.optimization_barrier((before, out_grad))
    turned = lax.ppermute(held_grad, ("seq", "ch"), route)

    padded = jnp.concatenate([before, features], axis=0).astype(F32)
    streams = [padded[:, i] for i in range(3)]
    filtered = []
    for i in range(3):
        total = jnp.zeros((rows, channels), F32)
        for j in range(taps):
            start = taps - 1 - j
            total = total + short_weight[i, j] * streams[i][start : start + rows]
        filtered.append(total)
    queries, keys, values = filtered
    product = (keys * values).astype(BF16).astype(F32)

    entry, total = local_states(product, rate, False)
    total, grad_pieces[2], grad_pieces[3] = lax.optimization_barrier(
        (total, grad_pieces[2], grad_pieces[3])
    )
    def weight_block(mask):
        return lax.dynamic_slice_in_dim(out_weight, (ch ^ mask) * width, width, 1)

    mixed_grad = jnp.zeros((rows, channels), F32)
    for mask in range(4):
        mixed_grad = mixed_grad + lax.dot_general(
            grad_pieces[mask],
            weight_block(mask),
            (((1,), (1,)), ((), ())),
            preferred_element_type=F32,
        )
    gate_grad = (mixed_grad * queries).astype(BF16).astype(F32)
    back_entry, back_total = local_states(gate_grad, rate, True)
    incoming, back_incoming = entering(jnp.stack([total, back_total]), rate, rows)

    gated = forward_apply(product, rate, amp, skip, entry, incoming).astype(BF16).astype(F32)
    mixed_out = (queries * gated).astype(BF16)
    query_grad = mixed_grad * gated

    def out_block(mask):
        return jnp.dot(mixed_out, weight_block(mask), preferred_element_type=F32)

    sent = jnp.concatenate([out_block(1).astype(BF16), out_block(3).astype(BF16)], axis=0)
    back_incoming, sent = lax.optimization_barrier((back_incoming, sent))
    got = flip_ch(sent, 1).astype(F32)
    far_sent = (out_block(2) + got[rows:]).astype(BF16)

    turned_pieces = jnp.concatenate(gather_ch(turned), axis=0)
    y_here = digit("y")
    around = jnp.stack([mixed_out] + [swap(mixed_out, "y", k) for k in (1, 2, 3)], axis=0)
    mixed_pieces = jnp.concatenate(
        [
            lax.dynamic_index_in_dim(around, y_here ^ ch ^ mask, 0, False)
            for mask in range(4)
        ],
        axis=0,
    )

    back, dots = backward_apply(gate_grad, product, rate, amp, skip, back_entry, back_incoming)
    back, far_sent = lax.optimization_barrier((back, far_sent))
    far = flip_ch(far_sent, 2)
    back = back.astype(BF16).astype(F32)
    filtered_grad = [query_grad, back * values, back * keys]
    edge = from_behind(jnp.stack([g[: taps - 1] for g in filtered_grad]), -1)
    feature_grad = []
    short_terms = []
    for i in range(3):
        padded_grad = jnp.concatenate([filtered_grad[i], edge[i]], axis=0)
        grad = jnp.zeros((rows, channels), F32)
        for j in range(taps):
            start = taps - 1 - j
            grad = grad + short_weight[i, j] * padded_grad[j : j + rows]
            short_terms.append(jnp.sum(filtered_grad[i] * streams[i][start : start + rows], axis=0))
        feature_grad.append(grad.astype(BF16))
    modes = rate.shape[0]
    parts = jnp.concatenate([dots, jnp.stack(short_terms)], axis=0)
    share = lax.dot_general(
        turned_pieces, mixed_pieces, (((0,), (0,)), ((), ())), preferred_element_type=F32
    ).astype(BF16)
    parts, share = lax.optimization_barrier((parts, share))
    groups = [[16 * y + i for i in range(16)] for y in range(4)]
    shares = lax.all_to_all(
        share, "seq", split_axis=0, concat_axis=0, axis_index_groups=groups, tiled=True
    )
    weight_grad = (
        jnp.sum(shares.reshape(16, width // 16, channels).astype(F32), axis=0) * grad_scale
    ).astype(BF16)
    sums = sum_along(parts, "y")
    sums, far = lax.optimization_barrier((sums, far))
    block_out = (out_block(0) + got[:rows] + far.astype(F32)).astype(BF16)
    sums = sum_along(sums, "x")
    sums = sum_along(sums, "z")
    residue_grad = (sums[:modes] * norm * grad_scale).T
    skip_grad = sums[modes] * grad_scale
    short_grad = (sums[modes + 1 :] * grad_scale).reshape(3, taps, channels)
    return (
        block_out,
        jnp.stack(feature_grad, axis=1),
        short_grad,
        residue_grad,
        skip_grad,
        weight_grad,
    )


def solution(mesh):
    in_specs = (
        P("seq", None, "ch"),
        P(None, None, "ch"),
        P("ch", None),
        P("ch", None),
        P("ch"),
        P("ch", None),
        P("seq", "ch"),
    )
    out_specs = (
        P("seq", "ch"),
        P("seq", None, "ch"),
        P(None, None, "ch"),
        P("ch", None),
        P("ch"),
        P("seq", "ch"),
    )
    return jax.shard_map(body, mesh=mesh, in_specs=in_specs, out_specs=out_specs, check_vma=False)
```
